256 devices in a mesh: tm: 32 (over z, y_hi, core), space: 8 (over y_lo, x).
Axes of the slice: x: 4, y: 4 (y_hi: 2, y_lo: 2; y = y_hi * 2 + y_lo), z: 8, core: 2. Of those that a mesh axis runs over, the one named last changes fastest.
Arguments:
- model: float32 [32, 8192, 1024], P('tm', 'space'), may hold values from -6 to 6
- kernels: float32 [3, 600, 8192], P(None, None, ('space', 'tm')), may hold values from -0.0390625 to 0.0390625
Outputs:
- data: float32 [32, 600, 1024], P('tm', None, 'space')
The draws below stay inside these ranges and needn't reach their ends.
All inputs are finite; a program needn't handle non-finite values.
Results may differ from the reference program's by a relative error of at most 0.0003.
Values sent between devices are 32-bit elements; how exact they have to be, the bound alone decides.
A program may use at most 64 MiB of HBM per device.

```python
import jax
import jax.numpy as jnp
from jax import lax

S = 600
COLS = 1024
LAGS = 3
TIMES = 32
P_SIZE = 8192


def raised(values, rng, source, target, parts, factor):
    owner, partner = [(jnp.arange(values.shape[position]) // (values.shape[position] // parts)).reshape([-1 if axis == position else 1 for axis in range(values.ndim)]) for position in (source, target)]
    chosen = jax.random.permutation(rng, parts)[partner]
    strong = (owner == chosen) | (owner == (partner + parts // 2) % parts)
    return jnp.where(strong, factor * values, values)


def block_levels(key, dims, split, smallest, top_value):
    level = 1.0
    for position, shards_of in split:
        steps = jax.random.uniform(jax.random.fold_in(jax.random.fold_in(key, 6), position), (shards_of,), jnp.float32, smallest / len(split), top_value / len(split))
        level = level * jnp.repeat(jnp.exp(steps), dims[position] // shards_of).reshape((-1,) + (1,) * (len(dims) - 1 - position))
    return level


def noise(rng, dims, deviation, limit, cuts=(), kind=jnp.bfloat16):
    drawn = jax.random.normal(rng, dims, jnp.float32) * deviation
    if len(cuts) > 0:
        drawn = block_levels(rng, dims, cuts, -0.22, 0.18) * drawn
    return jnp.clip(drawn, min=-limit, max=limit).astype(kind)


def noise_with(key, shape, deviation, most, pieces, heavy, kind=jnp.bfloat16):
    values = deviation * jax.random.normal(key, shape, jnp.float32)
    if pieces:
        values = values * block_levels(key, shape, pieces, -0.22, 0.18)
    return jnp.clip(raised(values, jax.random.fold_in(key, 3), *heavy), -most, most).astype(kind)


def setup_inputs(seed: int = 0) -> dict:
    arg_keys = jax.random.split(jax.random.key(seed), 3)
    model = noise_with(arg_keys[0], (TIMES, P_SIZE, COLS), 1.0, 6.0, ((0, 32), (1, 8)), (1, 2, 8, 2.0), jnp.float32)
    kernels = noise(arg_keys[1], (LAGS, S, P_SIZE), (LAGS * P_SIZE) ** -0.5, 0.0390625, ((2, 256),), jnp.float32)
    return {"model": model, "kernels": kernels}


def reference(model, kernels):
    def one_time(time_index):
        summed = jnp.zeros((S, COLS), jnp.float32)
        for lag_index in range(LAGS):
            source_time = jnp.maximum(time_index - lag_index, 0).astype(jnp.int32)
            model_block = lax.dynamic_index_in_dim(model, source_time, 0, keepdims=False)
            lag_term = jnp.dot(kernels[lag_index], model_block, precision=lax.Precision.HIGHEST, preferred_element_type=jnp.float32)
            summed = summed + jnp.where(time_index >= lag_index, lag_term, jnp.zeros_like(lag_term))
        return summed
    return lax.map(one_time, jnp.arange(TIMES, dtype=jnp.int32))
```

```python
import functools

import jax
import jax.numpy as jnp
from jax import lax
from jax.experimental import pallas as pl
from jax.experimental.pallas import tpu as pltpu
from jax.sharding import PartitionSpec as P

NZ, NX = 8, 4
CHUNKS, ROWS = 5, 120
LAGS = 3
MESH = pl.DeviceIdType.MESH
F32, BF16 = jnp.float32, jnp.bfloat16


def kernel(
    m_hbm, k_ref, out_ref,
    m_buf, k_pad, kbuf, kt_hi, kt_lo, w_hi, w_lo, pbuf, p1s, p1r, r1, r2, r3,
    m_sem, ky_s, ky_r, kz_s, kz_r, kf_s, kf_r, p1_s, p1_rs, r1_s, r1_r, r2_s, r2_r, r3_s, r3_r,
):
    tm, space = lax.axis_index("tm"), lax.axis_index("space")
    z, yh, c = tm // 4, (tm // 2) % 2, tm % 2
    yl, x = space // NX, space % NX

    def at_z(step):
        return ((z + step + NZ) % NZ * 4 + yh * 2 + c, space)

    def at_x(step):
        return (tm, yl * NX + (x + step + NX) % NX)

    other_yh = (z * 4 + (1 - yh) * 2 + c, space)
    other_core = (z * 4 + yh * 2 + (1 - c), space)
    other_yl = (tm, (1 - yl) * NX + x)
    later, earlier = (tm + 2) % 32, (tm + 30) % 32
    has_later, has_earlier = tm < 30, tm >= 2

    barrier = pltpu.get_barrier_semaphore()
    greeted = [
        at_z(1), at_z(-1), at_x(1), at_x(-1), other_yh, other_core, other_yl,
        (later, space), (later, other_yl[1]), (earlier, space), (earlier, other_yl[1]),
    ]
    for device in greeted:
        pl.semaphore_signal(barrier, inc=1, device_id=device, device_id_type=MESH)

    def load_model(i):
        rows = pl.ds(i * 256, 256)
        return pltpu.make_async_copy(m_hbm.at[rows], m_buf.at[rows], m_sem.at[i])

    for i in range(4):
        load_model(i).start()
    k_pad[...] = jnp.zeros_like(k_pad)
    for lag in range(LAGS):
        k_pad[lag, :, 0:600] = k_ref[lag]
    for lag in range(LAGS):
        whole = k_pad[lag]
        for j in range(CHUNKS):
            moved = whole if j == 0 else pltpu.roll(whole, 640 - ROWS * j, 1)
            kbuf[j, lag, c * NZ + z, yh] = moved[:, 0:128]
    pl.semaphore_wait(barrier, len(greeted))

    def remote(src, dst, send, recv, device):
        return pltpu.make_async_remote_copy(
            src_ref=src, dst_ref=dst, send_sem=send, recv_sem=recv, device_id=device, device_id_type=MESH
        )

    def over_yh(j, half):
        block = kbuf.at[j, :, c * NZ + z, half]
        return remote(block, block, ky_s.at[j], ky_r.at[j], other_yh)

    def over_z(j, hop, direction, source):
        sign = 1 - 2 * direction
        index = c * NZ + (z - sign * (source) + NZ) % NZ
        block = kbuf.at[j, :, index] if hop < 4 else kbuf.at[j, :, index, direction]
        return remote(block, block, kz_s.at[j, direction, hop - 1], kz_r.at[j, direction, hop - 1], at_z(sign))

    def send_z(j, hop, direction):
        return over_z(j, hop, direction, hop - 1)

    def recv_z(j, hop, direction):
        return over_z(j, hop, direction, hop)

    def to_core(j, core, hop, direction):
        sign = 1 - 2 * direction
        index = core * NZ + (z - sign * hop + NZ) % NZ
        block = kbuf.at[j, :, index] if hop < 4 else kbuf.at[j, :, index, direction]
        slot = 0 if hop == 0 else 2 * hop - 1 + direction
        return remote(block, block, kf_s.at[j, slot], kf_r.at[j, slot], other_core)

    hops = [(0, 0)] + [(hop, direction) for hop in (1, 2, 3, 4) for direction in (0, 1)]

    def advance(j, hop):
        if hop == 1:
            over_yh(j, 1 - yh).wait_recv()
            for direction in (0, 1):
                send_z(j, 1, direction).start()
            to_core(j, c, 0, 0).start()
        else:
            for direction in (0, 1):
                recv_z(j, hop - 1, direction).wait_recv()
                if hop <= 4:
                    send_z(j, hop, direction).start()
                to_core(j, c, hop - 1, direction).start()

    def swap_core(j, slot):
        return remote(p1s.at[j, slot], p1r.at[j, slot], p1_s.at[j, slot], p1_rs.at[j, slot], other_core)

    def first_x(j, direction):
        return remote(
            pbuf.at[j, 0, direction], r1.at[j, direction], r1_s.at[j, direction], r1_r.at[j, direction],
            at_x(1 - 2 * direction),
        )

    def second_x(j, direction):
        return remote(
            pbuf.at[j, 1 + direction], r2.at[j, direction], r2_s.at[j, direction], r2_r.at[j, direction],
            at_x(1 - 2 * direction),
        )

    def last(j, which):
        src = (pbuf.at[j, 3, 1 - yl, 0], pbuf.at[j, 3, yl, 1], pbuf.at[j, 3, 1 - yl, 1])[which]
        device = (other_yl, (later, space), (later, other_yl[1]))[which]
        return remote(src, r3.at[j, which], r3_s.at[j, which], r3_r.at[j, which], device)

    def transpose_chunk(j):
        def block(b, carry):
            for lag in range(LAGS):
                part = kbuf[j, lag, pl.ds(2 * b, 2)].reshape(128, 128).T
                high = part.astype(BF16)
                low = (part - high.astype(F32)).astype(BF16)
                columns = pl.ds(pl.multiple_of(b * 128, 128), 128)
                kt_hi[lag * 128 : (lag + 1) * 128, columns] = high
                kt_lo[lag * 128 : (lag + 1) * 128, columns] = low
            return carry

        lax.fori_loop(0, NZ, block, 0)

    def multiply(j, slot):
        to = (x + (2, 1, 3, 0)[slot]) % NX
        wide = w_hi[to]
        acc = jnp.dot(kt_hi[...], wide, preferred_element_type=F32)
        acc = acc + jnp.dot(kt_lo[...], wide, preferred_element_type=F32)
        acc = acc + jnp.dot(kt_hi[...], w_lo[to], preferred_element_type=F32)
        for half in (0, 1):
            lanes = slice(half * 128, half * 128 + 128)
            pbuf[j, slot, half, 0] = acc[0:ROWS, lanes]
            p1s[j, slot, half] = acc[128 : 128 + ROWS, lanes]
            pbuf[j, slot, half, 1] = acc[256 : 256 + ROWS, lanes]
        swap_core(j, slot).start()

    def combine(j, slot):
        swap_core(j, slot).wait_recv()
        for half in (0, 1):
            pbuf[j, slot, half, 1 - c] += p1r[j, slot, half]

    for j in range(CHUNKS):
        over_yh(j, yh).start()

    for i in range(4):
        load_model(i).wait()

    def split_rows(t, carry):
        rows = m_buf[pl.ds(pl.multiple_of(t * 32, 32), 32), :]
        high = rows.astype(BF16)
        low = (rows - high.astype(F32)).astype(BF16)
        to = pl.ds(pl.multiple_of(((t % 2) * NZ + t // 4) * 64 + (t // 2) % 2 * 32, 32), 32)
        for d in range(NX):
            for half in (0, 1):
                lanes = slice(half * 128, half * 128 + 128)
                columns = slice(half * 512 + d * 128, half * 512 + d * 128 + 128)
                w_hi[d, to, lanes] = high[:, columns]
                w_lo[d, to, lanes] = low[:, columns]
        return carry

    lax.fori_loop(0, 32, split_rows, 0)

    def iteration(i, carry):
        def on(offset):
            return (i - offset >= 0) & (i - offset < CHUNKS)

        @pl.when(on(0))
        def _():
            advance(i, 1)

        @pl.when(on(2))
        def _():
            advance(i - 2, 5)

        @pl.when(on(1))
        def _():
            advance(i - 1, 3)

        @pl.when(on(2))
        def _():
            j = i - 2
            for hop, direction in hops:
                to_core(j, 1 - c, hop, direction).wait_recv()
            transpose_chunk(j)
            multiply(j, 0)

        @pl.when(on(0))
        def _():
            advance(i, 2)

        @pl.when(on(2))
        def _():
            j = i - 2
            multiply(j, 1)
            combine(j, 0)
            for direction in (0, 1):
                first_x(j, direction).start()

        @pl.when(on(1))
        def _():
            advance(i - 1, 4)

        @pl.when(on(2))
        def _():
            j = i - 2
            multiply(j, 2)
            combine(j, 1)

        @pl.when(on(3))
        def _():
            j = i - 3
            for direction in (0, 1):
                first_x(j, direction).wait_recv()
                pbuf[j, 1 + direction, direction] += r1[j, direction]
                second_x(j, direction).start()

        @pl.when(on(2))
        def _():
            j = i - 2
            multiply(j, 3)
            combine(j, 2)
            combine(j, 3)

        @pl.when(on(4))
        def _():
            j = i - 4
            for direction in (0, 1):
                second_x(j, direction).wait_recv()
            pbuf[j, 3] = pbuf[j, 3] + r2[j, 0] + r2[j, 1]
            last(j, 0).start()

            @pl.when(has_later)
            def _():
                last(j, 1).start()
                last(j, 2).start()

        @pl.when(on(5))
        def _():
            j = i - 5
            last(j, 0).wait_recv()
            out_ref[j] = pbuf[j, 3, yl, 0] + r3[j, 0]

            @pl.when(has_earlier)
            def _():
                last(j, 1).wait_recv()
                last(j, 2).wait_recv()
                out_ref[j] = out_ref[j] + r3[j, 1] + r3[j, 2]

        return carry

    lax.fori_loop(0, CHUNKS + 5, iteration, 0)

    def drain(j, carry):
        over_yh(j, yh).wait_send()
        for direction in (0, 1):
            for hop in (1, 2, 3, 4):
                send_z(j, hop, direction).wait_send()
            first_x(j, direction).wait_send()
            second_x(j, direction).wait_send()
        for hop, direction in hops:
            to_core(j, c, hop, direction).wait_send()
        for slot in range(4):
            swap_core(j, slot).wait_send()
        last(j, 0).wait_send()

        @pl.when(has_later)
        def _():
            last(j, 1).wait_send()
            last(j, 2).wait_send()

        return carry

    lax.fori_loop(0, CHUNKS, drain, 0)


def on_device(model, kernels):
    dma = pltpu.SemaphoreType.DMA
    vmem = pltpu.VMEM
    result = pl.pallas_call(
        kernel,
        out_shape=jax.ShapeDtypeStruct((CHUNKS, ROWS, 128), F32),
        in_specs=[pl.BlockSpec(memory_space=pl.ANY), pl.BlockSpec(memory_space=pltpu.VMEM)],
        out_specs=pl.BlockSpec(memory_space=pltpu.VMEM),
        scratch_shapes=[
            vmem((1024, 1024), F32),
            vmem((LAGS, 32, 640), F32),
            vmem((CHUNKS, LAGS, 2 * NZ, 2, 32, 128), F32),
            vmem((LAGS * 128, 1024), BF16),
            vmem((LAGS * 128, 1024), BF16),
            vmem((NX, 1024, 256), BF16),
            vmem((NX, 1024, 256), BF16),
            vmem((CHUNKS, 4, 2, 2, ROWS, 128), F32),
            vmem((CHUNKS, 4, 2, ROWS, 128), F32),
            vmem((CHUNKS, 4, 2, ROWS, 128), F32),
            vmem((CHUNKS, 2, 2, ROWS, 128), F32),
            vmem((CHUNKS, 2, 2, 2, ROWS, 128), F32),
            vmem((CHUNKS, 3, ROWS, 128), F32),
            dma((4,)),
            dma((CHUNKS,)), dma((CHUNKS,)),
            dma((CHUNKS, 2, 4)), dma((CHUNKS, 2, 4)),
            dma((CHUNKS, 9)), dma((CHUNKS, 9)),
            dma((CHUNKS, 4)), dma((CHUNKS, 4)),
            dma((CHUNKS, 2)), dma((CHUNKS, 2)),
            dma((CHUNKS, 2)), dma((CHUNKS, 2)),
            dma((CHUNKS, 3)), dma((CHUNKS, 3)),
        ],
        compiler_params=pltpu.CompilerParams(
            collective_id=0, has_side_effects=True, vmem_limit_bytes=60 * 1024 * 1024
        ),
        name="toeplitz",
    )(model[0], jnp.swapaxes(kernels, 1, 2))
    return result.reshape(1, CHUNKS * ROWS, 128)


def solution(mesh):
    return jax.shard_map(
        on_device,
        mesh=mesh,
        in_specs=(P("tm", "space", None), P(None, None, ("space", "tm"))),
        out_specs=P("tm", None, "space"),
        check_vma=False,
    )
```

```python
import functools

import jax
import jax.numpy as jnp
from jax import lax
from jax.experimental import pallas as pl
from jax.experimental.pallas import tpu as pltpu
from jax.sharding import PartitionSpec as P

NZ, NX = 8, 4
LAGS, UNIT, UNITS = 3, 40, 15
MESH = pl.DeviceIdType.MESH
F32, BF16 = jnp.float32, jnp.bfloat16

SIZES = (1, 1, 2, 1, 3, 1, 3, 2, 1)
GATHER = "gcccgcccc"
REDUCE = "ddxddyyxx"
ORDER = (
    ("Y", 0), ("H1", 0), ("Y", 1), ("S", 0), ("Y", 2), ("Y", 3), ("Y", 4), ("H1", 4), ("Y", 5), ("H2", 0), ("H1", 1),
    ("Y", 6), ("H1", 2), ("Y", 7), ("Y", 8), ("H1", 3), ("H3", 0), ("H2", 1), ("H2", 4), ("H2", 2), ("H4", 0),
    ("H2", 3), ("H3", 1), ("H3", 4), ("H3", 2), ("H5", 0), ("H3", 3), ("H4", 1), ("H1", 5), ("H4", 4), ("H4", 2),
    ("F", 0), ("H1", 6), ("F", 1), ("T", 0), ("H4", 3), ("H5", 4), ("C0", 0), ("H2", 5), ("C1", 0), ("F", 2),
    ("C2", 0), ("H1", 7), ("C3", 0), ("T", 1), ("X0", 0), ("R1", 0), ("X1", 0), ("C0", 1), ("H2", 6), ("C1", 1),
    ("C2", 1), ("F", 3), ("X2", 0), ("R2", 0), ("X3", 0), ("C3", 1), ("F", 4), ("X0", 1), ("X1", 1), ("T", 2),
    ("H3", 5), ("R1", 1), ("X2", 1), ("X3", 1), ("C0", 2), ("H2", 7), ("C1", 2), ("R2", 1), ("C2", 2), ("H3", 6),
    ("C3", 2), ("R3", 0), ("X0", 2), ("R1", 2), ("X1", 2), ("T", 3), ("X2", 2), ("C0", 3), ("H4", 5), ("X3", 2),
    ("H1", 8), ("C1", 3), ("C2", 3), ("H3", 7), ("C3", 3), ("X0", 3), ("R1", 3), ("T", 4), ("H4", 6), ("R3", 1),
    ("X1", 3), ("X2", 3), ("R2", 3), ("F", 5), ("X3", 3), ("C0", 4), ("H2", 8), ("O", 0), ("R2", 2), ("C1", 4),
    ("H4", 7), ("C2", 4), ("F", 6), ("X0", 4), ("C3", 4), ("R3", 3), ("H3", 8), ("R1", 4), ("X1", 4), ("X2", 4),
    ("O", 1), ("T", 5), ("C0", 5), ("F", 7), ("C1", 5), ("C2", 5), ("C3", 5), ("R3", 2), ("X3", 4), ("X0", 5),
    ("T", 6), ("H4", 8), ("X1", 5), ("X2", 5), ("X3", 5), ("C0", 6), ("O", 3), ("R2", 4), ("C1", 6), ("C2", 6),
    ("X0", 6), ("C3", 6), ("F", 8), ("X1", 6), ("V0", 5), ("T", 7), ("O", 2), ("V1", 5), ("X2", 6), ("X3", 6),
    ("C0", 7), ("R1", 5), ("V2", 5), ("C1", 7), ("V3", 5), ("C2", 7), ("X0", 7), ("R1", 7), ("C3", 7), ("R3", 4),
    ("V0", 6), ("R1", 6), ("X1", 7), ("X2", 7), ("T", 8), ("C0", 8), ("X3", 7), ("R2", 5), ("C1", 8), ("C2", 8),
    ("C3", 8), ("V1", 6), ("X0", 8), ("R1", 8), ("D", 0), ("R2", 7), ("X1", 8), ("X2", 8), ("D", 1), ("X3", 8),
    ("D", 2), ("D", 3), ("V2", 6), ("R3", 5), ("R2", 6), ("V3", 6), ("R3", 7), ("R2", 8), ("R3", 6), ("O", 4),
    ("D", 4), ("O", 5), ("D", 5), ("R3", 8), ("O", 7), ("O", 6), ("D", 6), ("D", 7), ("O", 8), ("D", 8),
)
STARTS = tuple(sum(SIZES[:k]) for k in range(len(SIZES)))


def kernel(
    m_hbm, k_ref, out_ref,
    m_buf, k_pad, kbuf, kt_hi, kt_lo, w_hi, w_lo, pbuf, p1s, p1r, r0, r1, r2, r3, ry,
    m_sem, ky_s, ky_r, kz_s, kz_r, kf_s, kf_r, p1_s, p1_rs, r1_s, r1_r, r2_s, r2_r, r3_s, r3_r, ry_s, ry_r, kg_s, kg_r, kd_s, kd_r,
):
    tm, space = lax.axis_index("tm"), lax.axis_index("space")
    z, yh, c = tm // 4, (tm // 2) % 2, tm % 2
    yl, x = space // NX, space % NX

    def at_z(step):
        return ((z + step + NZ) % NZ * 4 + yh * 2 + c, space)

    def at_x(step):
        return (tm, yl * NX + (x + step + NX) % NX)

    other_yh = (z * 4 + (1 - yh) * 2 + c, space)
    other_core = (z * 4 + yh * 2 + (1 - c), space)
    other_yl = (tm, (1 - yl) * NX + x)
    later, earlier = (tm + 2) % 32, (tm + 30) % 32
    has_later, has_earlier = tm < 30, tm >= 2
    mine = c * NZ

    barrier = pltpu.get_barrier_semaphore()
    greeted = [
        (later, space), (later, other_yl[1]), (earlier, space), (earlier, other_yl[1]),
        at_z(1), at_z(-1), at_x(1), at_x(-1), other_yh, other_core, other_yl,
    ]
    if "d" in GATHER:
        greeted = [at_z(4), at_z(3), at_z(-3), at_z(2), at_z(-2)] + greeted
    if "d" in REDUCE:
        greeted = [at_x(2)] + greeted
    for device in greeted:
        pl.semaphore_signal(barrier, inc=1, device_id=device, device_id_type=MESH)

    def load_model(i):
        rows = pl.ds(i * 256, 256)
        return pltpu.make_async_copy(m_hbm.at[rows], m_buf.at[rows], m_sem.at[i])

    for i in range(4):
        load_model(i).start()

    k_pad[...] = jnp.zeros_like(k_pad)
    for lag in range(LAGS):
        k_pad[lag, :, 0:600] = k_ref[lag]
    lane = lax.broadcasted_iota(jnp.int32, (32, 128), 1)
    for u in range(UNITS):
        base = min(UNIT * u // 128 * 128, 384)
        parts = []
        for lag in range(LAGS):
            shift = (UNIT * lag - (UNIT * u - base)) % 256
            wide = k_pad[lag, :, base : base + 256]
            parts.append((pltpu.roll(wide, shift, 1) if shift else wide)[:, 0:128])
        tile = jnp.where(lane < UNIT, parts[0], jnp.where(lane < 2 * UNIT, parts[1], parts[2]))
        kbuf[u, mine + z, yh] = tile
    pl.semaphore_wait(barrier, len(greeted))

    def remote(src, dst, send, recv, device):
        return pltpu.make_async_remote_copy(
            src_ref=src, dst_ref=dst, send_sem=send, recv_sem=recv, device_id=device, device_id_type=MESH
        )

    def units(k):
        return pl.ds(STARTS[k], SIZES[k])

    def rows(k):
        return pl.ds(STARTS[k] * UNIT, SIZES[k] * UNIT)

    def over_yh(k, half):
        block = kbuf.at[units(k), mine + z, half]
        return remote(block, block, ky_s.at[k], ky_r.at[k], other_yh)

    def over_z(k, hop, direction, source):
        sign = 1 - 2 * direction
        index = mine + (z - sign * source + NZ) % NZ
        if GATHER[k] == "g":
            block = kbuf.at[units(k), index, yh]
        else:
            block = kbuf.at[units(k), index] if hop < 4 else kbuf.at[units(k), index, direction]
        return remote(block, block, kz_s.at[k, direction, hop - 1], kz_r.at[k, direction, hop - 1], at_z(sign))

    def ring_over_yh(k, hop, direction, half):
        index = mine + (z - (1 - 2 * direction) * hop + NZ) % NZ
        block = kbuf.at[units(k), index, half]
        return remote(block, block, kg_s.at[k, direction, hop - 1], kg_r.at[k, direction, hop - 1], other_yh)

    def straight(k, mirrored, step, source, half):
        block = kbuf.at[units(k), mine + (z - source + NZ) % NZ, half]
        return remote(block, block, kd_s.at[k, mirrored, step - 1], kd_r.at[k, mirrored, step - 1], at_z(step))

    def ring_hops(k):
        return [(hop, direction) for hop in (1, 2, 3) for direction in (0, 1)] + [(4, k % 2)]

    def to_core(k, core):
        block = kbuf.at[units(k), pl.ds(core * NZ, NZ)]
        return remote(block, block, kf_s.at[k], kf_r.at[k], other_core)

    def swap_core(k, slot):
        return remote(
            p1s.at[slot, :, rows(k)], p1r.at[slot, :, rows(k)], p1_s.at[k, slot], p1_rs.at[k, slot], other_core
        )

    def over_yl(k, slot):
        return remote(
            pbuf.at[slot, 1 - yl, :, rows(k)], ry.at[slot, :, rows(k)], ry_s.at[k, slot], ry_r.at[k, slot], other_yl
        )

    def first_x(k, direction):
        if REDUCE[k] == "y":
            src, dst = pbuf.at[0, yl, direction, rows(k)], r1.at[direction, 0, rows(k)]
        else:
            src, dst = pbuf.at[0, direction, :, rows(k)], r1.at[direction, :, rows(k)]
        return remote(src, dst, r1_s.at[k, direction], r1_r.at[k, direction], at_x(1 - 2 * direction))

    def far_x(k):
        return remote(pbuf.at[0, :, :, rows(k)], r0.at[:, :, rows(k)], r1_s.at[k, 0], r1_r.at[k, 0], at_x(2))

    def second_x(k, direction):
        if REDUCE[k] == "y":
            src, dst = pbuf.at[1 + direction, yl, :, rows(k)], r2.at[direction, 0, :, rows(k)]
        else:
            src, dst = pbuf.at[1 + direction, :, :, rows(k)], r2.at[direction, :, :, rows(k)]
        return remote(src, dst, r2_s.at[k, direction], r2_r.at[k, direction], at_x(1 - 2 * direction))

    def last(k, which):
        src = (
            pbuf.at[3, 1 - yl, 0, rows(k)], pbuf.at[3, yl, 1, rows(k)], pbuf.at[3, 1 - yl, 1, rows(k)]
        )[which]
        device = (other_yl, (later, space), (later, other_yl[1]))[which]
        return remote(src, r3.at[which, rows(k)], r3_s.at[k, which], r3_r.at[k, which], device)

    def step_y(k):
        over_yh(k, yh).start()

    def step_h(k, hop):
        if GATHER[k] == "d":
            if hop == 2:
                over_yh(k, 1 - yh).wait_recv()
            for step in range(1, NZ):
                straight(k, hop - 1, step, 0, yh if hop == 1 else 1 - yh).start()
            return
        if GATHER[k] == "g":
            for direction in (0, 1):
                if (hop - 1, direction) in ring_hops(k):
                    over_z(k, hop - 1, direction, hop - 1).wait_recv()
                if (hop, direction) in ring_hops(k):
                    over_z(k, hop, direction, hop - 1).start()
                if (hop - 1, direction) in ring_hops(k):
                    ring_over_yh(k, hop - 1, direction, yh).start()
            return
        if hop == 1:
            over_yh(k, 1 - yh).wait_recv()
        for direction in (0, 1):
            if hop > 1:
                over_z(k, hop - 1, direction, hop - 1).wait_recv()
            over_z(k, hop, direction, hop - 1).start()

    def step_f(k):
        if GATHER[k] == "d":
            for mirrored in (0, 1):
                for step in range(1, NZ):
                    straight(k, mirrored, step, step, 1 - yh if mirrored else yh).wait_recv()
        elif GATHER[k] == "g":
            over_yh(k, 1 - yh).wait_recv()
            for hop, direction in ring_hops(k):
                ring_over_yh(k, hop, direction, 1 - yh).wait_recv()
        else:
            for direction in (0, 1):
                over_z(k, 4, direction, 4).wait_recv()
        to_core(k, c).start()

    def step_s(k):
        for i in range(4):
            load_model(i).wait()

        def split_rows(t, carry):
            part = m_buf[pl.ds(pl.multiple_of(t * 32, 32), 32), :]
            high = part.astype(BF16)
            low = (part - high.astype(F32)).astype(BF16)
            to = pl.ds(pl.multiple_of(((t % 2) * NZ + t // 4) * 64 + (t // 2) % 2 * 32, 32), 32)
            for d in range(NX):
                for half in (0, 1):
                    lanes = slice(half * 128, half * 128 + 128)
                    columns = slice(half * 512 + d * 128, half * 512 + d * 128 + 128)
                    w_hi[d, to, lanes] = high[:, columns]
                    w_lo[d, to, lanes] = low[:, columns]
            return carry

        lax.fori_loop(0, 32, split_rows, 0)

    def step_t(k):
        to_core(k, 1 - c).wait_recv()

        def block(b, carry):
            columns = pl.ds(pl.multiple_of(b * 128, 128), 128)
            for u in range(SIZES[k]):
                part = kbuf[STARTS[k] + u, pl.ds(2 * b, 2)].reshape(128, 128).T
                high = part.astype(BF16)
                low = (part - high.astype(F32)).astype(BF16)
                kt_hi[u * 128 : (u + 1) * 128, columns] = high
                kt_lo[u * 128 : (u + 1) * 128, columns] = low
            return carry

        lax.fori_loop(0, NZ, block, 0)

    def step_c(k, slot):
        to = (x + (2, 1, 3, 0)[slot]) % NX
        high, low, wide = kt_hi[0 : SIZES[k] * 128], kt_lo[0 : SIZES[k] * 128], w_hi[to]
        acc = jnp.dot(high, wide, preferred_element_type=F32)
        acc = acc + jnp.dot(low, wide, preferred_element_type=F32)
        acc = acc + jnp.dot(high, w_lo[to], preferred_element_type=F32)
        for u in range(SIZES[k]):
            at = (STARTS[k] + u) * UNIT
            for half in (0, 1):
                lanes = slice(half * 128, half * 128 + 128)
                pbuf[slot, half, 0, at : at + UNIT] = acc[u * 128 : u * 128 + UNIT, lanes]
                p1s[slot, half, at : at + UNIT] = acc[u * 128 + UNIT : u * 128 + 2 * UNIT, lanes]
                pbuf[slot, half, 1, at : at + UNIT] = acc[u * 128 + 2 * UNIT : u * 128 + 3 * UNIT, lanes]
        swap_core(k, slot).start()

    def step_x(k, slot):
        swap_core(k, slot).wait_recv()
        for half in (0, 1):
            pbuf[slot, half, 1 - c, rows(k)] += p1r[slot, half, rows(k)]
        if REDUCE[k] == "y":
            over_yl(k, slot).start()

    def step_v(k, slot):
        over_yl(k, slot).wait_recv()
        pbuf[slot, yl, :, rows(k)] += ry[slot, :, rows(k)]

    def step_r1(k):
        if REDUCE[k] == "d":
            far_x(k).start()
            return
        for direction in (0, 1):
            first_x(k, direction).start()

    def step_r2(k):
        for direction in (0, 1):
            if REDUCE[k] == "d":
                second_x(k, direction).start()
                continue
            first_x(k, direction).wait_recv()
            if REDUCE[k] == "y":
                pbuf[1 + direction, yl, direction, rows(k)] += r1[direction, 0, rows(k)]
            else:
                pbuf[1 + direction, direction, :, rows(k)] += r1[direction, :, rows(k)]
            second_x(k, direction).start()

    def step_r3(k):
        for direction in (0, 1):
            second_x(k, direction).wait_recv()
        if REDUCE[k] == "y":
            pbuf[3, yl, :, rows(k)] = pbuf[3, yl, :, rows(k)] + r2[0, 0, :, rows(k)] + r2[1, 0, :, rows(k)]
        else:
            total = pbuf[3, :, :, rows(k)] + r2[0, :, :, rows(k)] + r2[1, :, :, rows(k)]
            if REDUCE[k] == "d":
                far_x(k).wait_recv()
                total = total + r0[:, :, rows(k)]
            pbuf[3, :, :, rows(k)] = total
            last(k, 0).start()

        @pl.when(has_later)
        def _():
            last(k, 1).start()
            if REDUCE[k] != "y":
                last(k, 2).start()

    def step_o(k):
        total = pbuf[3, yl, 0, rows(k)]
        if REDUCE[k] != "y":
            last(k, 0).wait_recv()
            total = total + r3[0, rows(k)]
        out_ref[rows(k)] = total

        @pl.when(has_earlier)
        def _():
            last(k, 1).wait_recv()
            more = r3[1, rows(k)]
            if REDUCE[k] != "y":
                last(k, 2).wait_recv()
                more = more + r3[2, rows(k)]
            out_ref[rows(k)] += more

    def step_d(k):
        over_yh(k, yh).wait_send()
        if GATHER[k] == "d":
            for mirrored in (0, 1):
                for step in range(1, NZ):
                    straight(k, mirrored, step, 0, 1 - yh if mirrored else yh).wait_send()
        elif GATHER[k] == "g":
            for hop, direction in ring_hops(k):
                over_z(k, hop, direction, hop - 1).wait_send()
                ring_over_yh(k, hop, direction, yh).wait_send()
        else:
            for direction in (0, 1):
                for hop in (1, 2, 3, 4):
                    over_z(k, hop, direction, hop - 1).wait_send()
        if REDUCE[k] == "d":
            far_x(k).wait_send()
        for direction in (0, 1):
            if REDUCE[k] != "d":
                first_x(k, direction).wait_send()
            second_x(k, direction).wait_send()
        to_core(k, c).wait_send()
        for slot in range(4):
            swap_core(k, slot).wait_send()
            if REDUCE[k] == "y":
                over_yl(k, slot).wait_send()
        if REDUCE[k] != "y":
            last(k, 0).wait_send()

        @pl.when(has_later)
        def _():
            last(k, 1).wait_send()
            if REDUCE[k] != "y":
                last(k, 2).wait_send()

    steps = {
        "Y": step_y, "F": step_f, "S": step_s, "T": step_t, "R1": step_r1, "R2": step_r2, "R3": step_r3,
        "O": step_o, "D": step_d,
    }
    for hop in (1, 2, 3, 4, 5):
        steps[f"H{hop}"] = functools.partial(step_h, hop=hop)
    for slot in range(4):
        steps[f"C{slot}"] = functools.partial(step_c, slot=slot)
        steps[f"X{slot}"] = functools.partial(step_x, slot=slot)
        steps[f"V{slot}"] = functools.partial(step_v, slot=slot)
    for name, k in ORDER:
        steps[name](k)


def on_device(model, kernels):
    dma, vmem, n = pltpu.SemaphoreType.DMA, pltpu.VMEM, len(SIZES)
    result = pl.pallas_call(
        kernel,
        out_shape=jax.ShapeDtypeStruct((600, 128), F32),
        in_specs=[pl.BlockSpec(memory_space=pl.ANY), pl.BlockSpec(memory_space=pltpu.VMEM)],
        out_specs=pl.BlockSpec(memory_space=pltpu.VMEM),
        scratch_shapes=[
            vmem((1024, 1024), F32),
            vmem((LAGS, 32, 640), F32),
            vmem((UNITS, 2 * NZ, 2, 32, 128), F32),
            vmem((max(SIZES) * 128, 1024), BF16),
            vmem((max(SIZES) * 128, 1024), BF16),
            vmem((NX, 1024, 256), BF16),
            vmem((NX, 1024, 256), BF16),
            vmem((4, 2, 2, 600, 128), F32),
            vmem((4, 2, 600, 128), F32),
            vmem((4, 2, 600, 128), F32),
            vmem((2, 2, 600, 128), F32),
            vmem((2, 2, 600, 128), F32),
            vmem((2, 2, 2, 600, 128), F32),
            vmem((3, 600, 128), F32),
            vmem((4, 2, 600, 128), F32),
            dma((4,)),
            dma((n,)), dma((n,)),
            dma((n, 2, 4)), dma((n, 2, 4)),
            dma((n,)), dma((n,)),
            dma((n, 4)), dma((n, 4)),
            dma((n, 2)), dma((n, 2)),
            dma((n, 2)), dma((n, 2)),
            dma((n, 3)), dma((n, 3)),
            dma((n, 4)), dma((n, 4)),
            dma((n, 2, 4)), dma((n, 2, 4)),
            dma((n, 2, 7)), dma((n, 2, 7)),
        ],
        compiler_params=pltpu.CompilerParams(
            collective_id=0, has_side_effects=True, vmem_limit_bytes=60 * 1024 * 1024
        ),
        name="toeplitz",
    )(model[0], jnp.swapaxes(kernels, 1, 2))
    return result[None]


def solution(mesh):
    return jax.shard_map(
        on_device,
        mesh=mesh,
        in_specs=(P("tm", "space", None), P(None, None, ("space", "tm"))),
        out_specs=P("tm", None, "space"),
        check_vma=False,
    )
```

```python
import functools

import jax
import jax.numpy as jnp
from jax import lax
from jax.experimental import pallas as pl
from jax.experimental.pallas import tpu as pltpu
from jax.sharding import PartitionSpec as P

NZ, NX = 8, 4
LAGS, UNIT, UNITS = 3, 40, 15
MESH = pl.DeviceIdType.MESH
F32, BF16 = jnp.float32, jnp.bfloat16

SIZES = (2, 1, 3, 2, 3, 2, 2)
GATHER = "gcccccc"
REDUCE = "xxxyxxy"
ORDER = (
    ("Y", 0), ("H1", 0), ("Y", 1), ("S", 0), ("Y", 2), ("Y", 3), ("Y", 4), ("H2", 0), ("H1", 1), ("Y", 5), ("H1", 2),
    ("Y", 6), ("H3", 0), ("H1", 3), ("H2", 1), ("H2", 2), ("H4", 0), ("H2", 3), ("H3", 1), ("H3", 2), ("H5", 0),
    ("H1", 4), ("H3", 3), ("F", 0), ("H4", 1), ("H4", 2), ("H2", 4), ("T", 0), ("C0", 0), ("H4", 3), ("C1", 0),
    ("F", 1), ("H1", 6), ("C2", 0), ("F", 2), ("X0", 0), ("R1", 0), ("C3", 0), ("H1", 5), ("X1", 0), ("T", 1),
    ("X2", 0), ("C0", 1), ("H3", 4), ("C1", 1), ("F", 3), ("C2", 1), ("C3", 1), ("T", 2), ("R2", 0), ("H2", 6),
    ("X3", 0), ("X0", 1), ("R1", 1), ("X1", 1), ("C0", 2), ("H2", 5), ("X2", 1), ("X3", 1), ("C1", 2), ("H4", 4),
    ("C2", 2), ("X0", 2), ("R1", 2), ("C3", 2), ("H3", 6), ("X1", 2), ("T", 3), ("R3", 0), ("H3", 5), ("X3", 2),
    ("X2", 2), ("C0", 3), ("F", 4), ("C1", 3), ("R2", 1), ("C2", 3), ("X0", 3), ("H4", 6), ("C3", 3), ("R2", 2),
    ("H4", 5), ("T", 4), ("X1", 3), ("X2", 3), ("X3", 3), ("R3", 1), ("F", 6), ("O", 0), ("C0", 4), ("V0", 3),
    ("R1", 3), ("F", 5), ("C1", 4), ("C2", 4), ("X0", 4), ("R1", 4), ("C3", 4), ("R3", 2), ("V1", 3), ("X1", 4),
    ("X2", 4), ("T", 5), ("V2", 3), ("X3", 4), ("C0", 5), ("R2", 3), ("C1", 5), ("V3", 3), ("C2", 5), ("R2", 4),
    ("X0", 5), ("C3", 5), ("X1", 5), ("T", 6), ("R1", 5), ("X2", 5), ("O", 1), ("C0", 6), ("R3", 3), ("X3", 5),
    ("C1", 6), ("C2", 6), ("X0", 6), ("C3", 6), ("O", 2), ("X1", 6), ("D", 0), ("X2", 6), ("D", 1), ("D", 2),
    ("X3", 6), ("R3", 4), ("O", 3), ("D", 3), ("V0", 6), ("R1", 6), ("R2", 5), ("V1", 6), ("V2", 6), ("R2", 6),
    ("V3", 6), ("R3", 5), ("R3", 6), ("D", 4), ("D", 5), ("D", 6), ("E", 0), ("E", 1), ("E", 2), ("E", 3), ("O", 4),
    ("O", 5), ("O", 6), ("E", 4), ("E", 5), ("E", 6),
)
STARTS = tuple(sum(SIZES[:k]) for k in range(len(SIZES)))


def kernel(
    m_hbm, k_ref, out_ref,
    m_buf, k_pad, kbuf, kt_hi, kt_lo, w_hi, w_lo, pbuf, p1s, p1r, r0, r1, r2, r3, ry,
    m_sem, ky_s, ky_r, kz_s, kz_r, kf_s, kf_r, p1_s, p1_rs, r1_s, r1_r, r2_s, r2_r, r3_s, r3_r, ry_s, ry_r, kg_s, kg_r, kd_s, kd_r,
):
    tm, space = lax.axis_index("tm"), lax.axis_index("space")
    z, yh, c = tm // 4, (tm // 2) % 2, tm % 2
    yl, x = space // NX, space % NX

    def at_z(step):
        return ((z + step + NZ) % NZ * 4 + yh * 2 + c, space)

    def at_x(step):
        return (tm, yl * NX + (x + step + NX) % NX)

    other_yh = (z * 4 + (1 - yh) * 2 + c, space)
    other_core = (z * 4 + yh * 2 + (1 - c), space)
    other_yl = (tm, (1 - yl) * NX + x)
    later, earlier = (tm + 2) % 32, (tm + 30) % 32
    has_later, has_earlier = tm < 30, tm >= 2
    mine = c * NZ

    barrier = pltpu.get_barrier_semaphore()
    greeted = [
        (later, space), (later, other_yl[1]), (earlier, space), (earlier, other_yl[1]),
        at_z(1), at_z(-1), at_x(1), at_x(-1), other_yh, other_core, other_yl,
    ]
    if "d" in GATHER:
        greeted = [at_z(4), at_z(3), at_z(-3), at_z(2), at_z(-2)] + greeted
    if "d" in REDUCE:
        greeted = [at_x(2)] + greeted
    for device in greeted:
        pl.semaphore_signal(barrier, inc=1, device_id=device, device_id_type=MESH)

    def load_model(i):
        rows = pl.ds(i * 256, 256)
        return pltpu.make_async_copy(m_hbm.at[rows], m_buf.at[rows], m_sem.at[i])

    for i in range(4):
        load_model(i).start()

    k_pad[...] = jnp.zeros_like(k_pad)
    for lag in range(LAGS):
        k_pad[lag, :, 0:600] = k_ref[lag]
    lane = lax.broadcasted_iota(jnp.int32, (32, 128), 1)
    for u in range(UNITS):
        base = min(UNIT * u // 128 * 128, 384)
        parts = []
        for lag in range(LAGS):
            shift = (UNIT * lag - (UNIT * u - base)) % 256
            wide = k_pad[lag, :, base : base + 256]
            parts.append((pltpu.roll(wide, shift, 1) if shift else wide)[:, 0:128])
        tile = jnp.where(lane < UNIT, parts[0], jnp.where(lane < 2 * UNIT, parts[1], parts[2]))
        kbuf[u, mine + z, yh] = tile
    pl.semaphore_wait(barrier, len(greeted))

    def remote(src, dst, send, recv, device):
        return pltpu.make_async_remote_copy(
            src_ref=src, dst_ref=dst, send_sem=send, recv_sem=recv, device_id=device, device_id_type=MESH
        )

    def units(k):
        return pl.ds(STARTS[k], SIZES[k])

    def rows(k):
        return pl.ds(STARTS[k] * UNIT, SIZES[k] * UNIT)

    def over_yh(k, half):
        block = kbuf.at[units(k), mine + z, half]
        return remote(block, block, ky_s.at[k], ky_r.at[k], other_yh)

    def over_z(k, hop, direction, source):
        sign = 1 - 2 * direction
        index = mine + (z - sign * source + NZ) % NZ
        if GATHER[k] == "g":
            block = kbuf.at[units(k), index, yh]
        else:
            block = kbuf.at[units(k), index] if hop < 4 else kbuf.at[units(k), index, direction]
        return remote(block, block, kz_s.at[k, direction, hop - 1], kz_r.at[k, direction, hop - 1], at_z(sign))

    def ring_over_yh(k, hop, direction, half):
        index = mine + (z - (1 - 2 * direction) * hop + NZ) % NZ
        block = kbuf.at[units(k), index, half]
        return remote(block, block, kg_s.at[k, direction, hop - 1], kg_r.at[k, direction, hop - 1], other_yh)

    def straight(k, mirrored, step, source, half):
        block = kbuf.at[units(k), mine + (z - source + NZ) % NZ, half]
        return remote(block, block, kd_s.at[k, mirrored, step - 1], kd_r.at[k, mirrored, step - 1], at_z(step))

    def ring_hops(k):
        return [(hop, direction) for hop in (1, 2, 3) for direction in (0, 1)] + [(4, k % 2)]

    def to_core(k, core):
        block = kbuf.at[units(k), pl.ds(core * NZ, NZ)]
        return remote(block, block, kf_s.at[k], kf_r.at[k], other_core)

    def swap_core(k, slot):
        return remote(
            p1s.at[slot, :, rows(k)], p1r.at[slot, :, rows(k)], p1_s.at[k, slot], p1_rs.at[k, slot], other_core
        )

    def over_yl(k, slot):
        return remote(
            pbuf.at[slot, 1 - yl, :, rows(k)], ry.at[slot, :, rows(k)], ry_s.at[k, slot], ry_r.at[k, slot], other_yl
        )

    def first_x(k, direction):
        if REDUCE[k] == "y":
            src, dst = pbuf.at[0, yl, direction, rows(k)], r1.at[direction, 0, rows(k)]
        else:
            src, dst = pbuf.at[0, direction, :, rows(k)], r1.at[direction, :, rows(k)]
        return remote(src, dst, r1_s.at[k, direction], r1_r.at[k, direction], at_x(1 - 2 * direction))

    def far_x(k):
        return remote(pbuf.at[0, :, :, rows(k)], r0.at[:, :, rows(k)], r1_s.at[k, 0], r1_r.at[k, 0], at_x(2))

    def second_x(k, direction):
        if REDUCE[k] == "y":
            src, dst = pbuf.at[1 + direction, yl, :, rows(k)], r2.at[direction, 0, :, rows(k)]
        else:
            src, dst = pbuf.at[1 + direction, :, :, rows(k)], r2.at[direction, :, :, rows(k)]
        return remote(src, dst, r2_s.at[k, direction], r2_r.at[k, direction], at_x(1 - 2 * direction))

    def last(k, which):
        src = (
            pbuf.at[3, 1 - yl, 0, rows(k)], pbuf.at[3, yl, 1, rows(k)], pbuf.at[3, 1 - yl, 1, rows(k)]
        )[which]
        device = (other_yl, (later, space), (later, other_yl[1]))[which]
        return remote(src, r3.at[which, rows(k)], r3_s.at[k, which], r3_r.at[k, which], device)

    def step_y(k):
        over_yh(k, yh).start()

    def step_h(k, hop):
        if GATHER[k] == "d":
            if hop == 2:
                over_yh(k, 1 - yh).wait_recv()
            for step in range(1, NZ):
                straight(k, hop - 1, step, 0, yh if hop == 1 else 1 - yh).start()
            return
        if GATHER[k] == "g":
            for direction in (0, 1):
                if (hop - 1, direction) in ring_hops(k):
                    over_z(k, hop - 1, direction, hop - 1).wait_recv()
                if (hop, direction) in ring_hops(k):
                    over_z(k, hop, direction, hop - 1).start()
                if (hop - 1, direction) in ring_hops(k):
                    ring_over_yh(k, hop - 1, direction, yh).start()
            return
        if hop == 1:
            over_yh(k, 1 - yh).wait_recv()
        for direction in (0, 1):
            if hop > 1:
                over_z(k, hop - 1, direction, hop - 1).wait_recv()
            over_z(k, hop, direction, hop - 1).start()

    def step_f(k):
        if GATHER[k] == "d":
            for mirrored in (0, 1):
                for step in range(1, NZ):
                    straight(k, mirrored, step, step, 1 - yh if mirrored else yh).wait_recv()
        elif GATHER[k] == "g":
            over_yh(k, 1 - yh).wait_recv()
            for hop, direction in ring_hops(k):
                ring_over_yh(k, hop, direction, 1 - yh).wait_recv()
        else:
            for direction in (0, 1):
                over_z(k, 4, direction, 4).wait_recv()
        to_core(k, c).start()

    def step_s(k):
        for i in range(4):
            load_model(i).wait()

        def split_rows(t, carry):
            part = m_buf[pl.ds(pl.multiple_of(t * 32, 32), 32), :]
            high = part.astype(BF16)
            low = (part - high.astype(F32)).astype(BF16)
            to = pl.ds(pl.multiple_of(((t % 2) * NZ + t // 4) * 64 + (t // 2) % 2 * 32, 32), 32)
            for d in range(NX):
                for half in (0, 1):
                    lanes = slice(half * 128, half * 128 + 128)
                    columns = slice(half * 512 + d * 128, half * 512 + d * 128 + 128)
                    w_hi[d, to, lanes] = high[:, columns]
                    w_lo[d, to, lanes] = low[:, columns]
            return carry

        lax.fori_loop(0, 32, split_rows, 0)

    def step_t(k):
        to_core(k, 1 - c).wait_recv()

        def block(b, carry):
            columns = pl.ds(pl.multiple_of(b * 128, 128), 128)
            for u in range(SIZES[k]):
                part = kbuf[STARTS[k] + u, pl.ds(2 * b, 2)].reshape(128, 128).T
                high = part.astype(BF16)
                low = (part - high.astype(F32)).astype(BF16)
                kt_hi[u * 128 : (u + 1) * 128, columns] = high
                kt_lo[u * 128 : (u + 1) * 128, columns] = low
            return carry

        lax.fori_loop(0, NZ, block, 0)

    def step_c(k, slot):
        to = (x + (2, 1, 3, 0)[slot]) % NX
        high, low, wide = kt_hi[0 : SIZES[k] * 128], kt_lo[0 : SIZES[k] * 128], w_hi[to]
        acc = jnp.dot(high, wide, preferred_element_type=F32)
        acc = acc + jnp.dot(low, wide, preferred_element_type=F32)
        acc = acc + jnp.dot(high, w_lo[to], preferred_element_type=F32)
        for u in range(SIZES[k]):
            at = (STARTS[k] + u) * UNIT
            for half in (0, 1):
                lanes = slice(half * 128, half * 128 + 128)
                pbuf[slot, half, 0, at : at + UNIT] = acc[u * 128 : u * 128 + UNIT, lanes]
                p1s[slot, half, at : at + UNIT] = acc[u * 128 + UNIT : u * 128 + 2 * UNIT, lanes]
                pbuf[slot, half, 1, at : at + UNIT] = acc[u * 128 + 2 * UNIT : u * 128 + 3 * UNIT, lanes]
        swap_core(k, slot).start()

    def step_x(k, slot):
        swap_core(k, slot).wait_recv()
        for half in (0, 1):
            pbuf[slot, half, 1 - c, rows(k)] += p1r[slot, half, rows(k)]
        if REDUCE[k] == "y":
            over_yl(k, slot).start()

    def step_v(k, slot):
        over_yl(k, slot).wait_recv()
        pbuf[slot, yl, :, rows(k)] += ry[slot, :, rows(k)]

    def step_r1(k):
        if REDUCE[k] == "d":
            far_x(k).start()
            return
        for direction in (0, 1):
            first_x(k, direction).start()

    def step_r2(k):
        for direction in (0, 1):
            if REDUCE[k] == "d":
                second_x(k, direction).start()
                continue
            first_x(k, direction).wait_recv()
            if REDUCE[k] == "y":
                pbuf[1 + direction, yl, direction, rows(k)] += r1[direction, 0, rows(k)]
            else:
                pbuf[1 + direction, direction, :, rows(k)] += r1[direction, :, rows(k)]
            second_x(k, direction).start()

    def step_r3(k):
        for direction in (0, 1):
            second_x(k, direction).wait_recv()
        if REDUCE[k] == "y":
            pbuf[3, yl, :, rows(k)] = pbuf[3, yl, :, rows(k)] + r2[0, 0, :, rows(k)] + r2[1, 0, :, rows(k)]
        else:
            total = pbuf[3, :, :, rows(k)] + r2[0, :, :, rows(k)] + r2[1, :, :, rows(k)]
            if REDUCE[k] == "d":
                far_x(k).wait_recv()
                total = total + r0[:, :, rows(k)]
            pbuf[3, :, :, rows(k)] = total
            last(k, 0).start()

        @pl.when(has_later)
        def _():
            last(k, 1).start()
            if REDUCE[k] != "y":
                last(k, 2).start()

    def step_o(k):
        total = pbuf[3, yl, 0, rows(k)]
        if REDUCE[k] != "y":
            last(k, 0).wait_recv()
            total = total + r3[0, rows(k)]
        out_ref[rows(k)] = total

        @pl.when(has_earlier)
        def _():
            last(k, 1).wait_recv()
            more = r3[1, rows(k)]
            if REDUCE[k] != "y":
                last(k, 2).wait_recv()
                more = more + r3[2, rows(k)]
            out_ref[rows(k)] += more

    def step_d(k):
        over_yh(k, yh).wait_send()
        if GATHER[k] == "d":
            for mirrored in (0, 1):
                for step in range(1, NZ):
                    straight(k, mirrored, step, 0, 1 - yh if mirrored else yh).wait_send()
        elif GATHER[k] == "g":
            for hop, direction in ring_hops(k):
                over_z(k, hop, direction, hop - 1).wait_send()
                ring_over_yh(k, hop, direction, yh).wait_send()
        else:
            for direction in (0, 1):
                for hop in (1, 2, 3, 4):
                    over_z(k, hop, direction, hop - 1).wait_send()
        if REDUCE[k] == "d":
            far_x(k).wait_send()
        for direction in (0, 1):
            if REDUCE[k] != "d":
                first_x(k, direction).wait_send()
            second_x(k, direction).wait_send()
        to_core(k, c).wait_send()
        for slot in range(4):
            swap_core(k, slot).wait_send()
            if REDUCE[k] == "y":
                over_yl(k, slot).wait_send()

    def step_e(k):
        if REDUCE[k] != "y":
            last(k, 0).wait_send()

        @pl.when(has_later)
        def _():
            last(k, 1).wait_send()
            if REDUCE[k] != "y":
                last(k, 2).wait_send()

    steps = {
        "Y": step_y, "F": step_f, "S": step_s, "T": step_t, "R1": step_r1, "R2": step_r2, "R3": step_r3,
        "O": step_o, "D": step_d, "E": step_e,
    }
    for hop in (1, 2, 3, 4, 5):
        steps[f"H{hop}"] = functools.partial(step_h, hop=hop)
    for slot in range(4):
        steps[f"C{slot}"] = functools.partial(step_c, slot=slot)
        steps[f"X{slot}"] = functools.partial(step_x, slot=slot)
        steps[f"V{slot}"] = functools.partial(step_v, slot=slot)
    for name, k in ORDER:
        steps[name](k)


def on_device(model, kernels):
    dma, vmem, n = pltpu.SemaphoreType.DMA, pltpu.VMEM, len(SIZES)
    result = pl.pallas_call(
        kernel,
        out_shape=jax.ShapeDtypeStruct((600, 128), F32),
        in_specs=[pl.BlockSpec(memory_space=pl.ANY), pl.BlockSpec(memory_space=pltpu.VMEM)],
        out_specs=pl.BlockSpec(memory_space=pltpu.VMEM),
        scratch_shapes=[
            vmem((1024, 1024), F32),
            vmem((LAGS, 32, 640), F32),
            vmem((UNITS, 2 * NZ, 2, 32, 128), F32),
            vmem((max(SIZES) * 128, 1024), BF16),
            vmem((max(SIZES) * 128, 1024), BF16),
            vmem((NX, 1024, 256), BF16),
            vmem((NX, 1024, 256), BF16),
            vmem((4, 2, 2, 600, 128), F32),
            vmem((4, 2, 600, 128), F32),
            vmem((4, 2, 600, 128), F32),
            vmem((2, 2, 600, 128), F32),
            vmem((2, 2, 600, 128), F32),
            vmem((2, 2, 2, 600, 128), F32),
            vmem((3, 600, 128), F32),
            vmem((4, 2, 600, 128), F32),
            dma((4,)),
            dma((n,)), dma((n,)),
            dma((n, 2, 4)), dma((n, 2, 4)),
            dma((n,)), dma((n,)),
            dma((n, 4)), dma((n, 4)),
            dma((n, 2)), dma((n, 2)),
            dma((n, 2)), dma((n, 2)),
            dma((n, 3)), dma((n, 3)),
            dma((n, 4)), dma((n, 4)),
            dma((n, 2, 4)), dma((n, 2, 4)),
            dma((n, 2, 7)), dma((n, 2, 7)),
        ],
        compiler_params=pltpu.CompilerParams(
            collective_id=0, has_side_effects=True, vmem_limit_bytes=60 * 1024 * 1024
        ),
        name="toeplitz",
    )(model[0], jnp.swapaxes(kernels, 1, 2))
    return result[None]


def solution(mesh):
    return jax.shard_map(
        on_device,
        mesh=mesh,
        in_specs=(P("tm", "space", None), P(None, None, ("space", "tm"))),
        out_specs=P("tm", None, "space"),
        check_vma=False,
    )
```

```python
import functools

import jax
import jax.numpy as jnp
from jax import lax
from jax.experimental import pallas as pl
from jax.experimental.pallas import tpu as pltpu
from jax.sharding import PartitionSpec as P

NZ, NX = 8, 4
LAGS, UNIT, UNITS = 3, 40, 15
MESH = pl.DeviceIdType.MESH
F32, BF16 = jnp.float32, jnp.bfloat16

SIZES = (1, 2, 2, 1, 3, 3, 2, 1)
GATHER = "gcccgccc"
REDUCE = "dxxyxyxx"
ORDER = (
    ("Y", 0), ("Y", 1), ("H1", 0), ("S", 0), ("Y", 2), ("Y", 3), ("Y", 4), ("H1", 4), ("Y", 5), ("H2", 0), ("H1", 1),
    ("Y", 6), ("H1", 2), ("Y", 7), ("H1", 3), ("H3", 0), ("H2", 4), ("H2", 1), ("H1", 7), ("H2", 3), ("H4", 0),
    ("H2", 2), ("H3", 1), ("H3", 4), ("H5", 0), ("H3", 3), ("H3", 2), ("H4", 1), ("H1", 5), ("F", 0), ("H4", 3),
    ("H4", 2), ("H4", 4), ("F", 1), ("T", 0), ("H1", 6), ("C0", 0), ("C1", 0), ("C2", 0), ("H2", 5), ("C3", 0),
    ("F", 3), ("T", 1), ("F", 2), ("X0", 0), ("R1", 0), ("X1", 0), ("X2", 0), ("R2", 0), ("H5", 4), ("X3", 0),
    ("C0", 1), ("H2", 7), ("C1", 1), ("H2", 6), ("C2", 1), ("C3", 1), ("X0", 1), ("R1", 1), ("X1", 1), ("T", 2),
    ("H3", 5), ("X2", 1), ("C0", 2), ("F", 4), ("X3", 1), ("C1", 2), ("H3", 6), ("R3", 0), ("C2", 2), ("X0", 2),
    ("R1", 2), ("C3", 2), ("H3", 7), ("R2", 1), ("T", 3), ("C0", 3), ("H4", 5), ("X2", 2), ("X1", 2), ("C1", 3),
    ("X3", 2), ("C2", 3), ("C3", 3), ("H4", 6), ("T", 4), ("H4", 7), ("O", 0), ("R2", 2), ("X1", 3), ("C0", 4),
    ("F", 5), ("X0", 3), ("X2", 3), ("X3", 3), ("C1", 4), ("F", 6), ("R3", 1), ("X0", 4), ("R1", 4), ("C2", 4),
    ("F", 7), ("V1", 3), ("C3", 4), ("T", 5), ("R3", 2), ("X1", 4), ("V0", 3), ("R1", 3), ("X2", 4), ("V2", 3),
    ("V3", 3), ("C0", 5), ("X3", 4), ("C1", 5), ("R2", 4), ("C2", 5), ("X0", 5), ("O", 1), ("C3", 5), ("R2", 3),
    ("X1", 5), ("X2", 5), ("T", 6), ("O", 2), ("C0", 6), ("X3", 5), ("C1", 6), ("C2", 6), ("C3", 6), ("X0", 6),
    ("R1", 6), ("V0", 5), ("R1", 5), ("T", 7), ("R3", 4), ("X2", 6), ("C0", 7), ("C1", 7), ("X1", 6), ("V1", 5),
    ("X3", 6), ("C2", 7), ("R3", 3), ("X0", 7), ("R1", 7), ("C3", 7), ("X1", 7), ("D", 0), ("D", 1), ("R2", 6),
    ("X2", 7), ("D", 2), ("V2", 5), ("X3", 7), ("R2", 5), ("R2", 7), ("V3", 5), ("R3", 6), ("O", 4), ("R3", 5),
    ("O", 3), ("D", 3), ("D", 4), ("R3", 7), ("D", 5), ("D", 6), ("D", 7), ("E", 0), ("E", 1), ("E", 2), ("E", 3),
    ("E", 4), ("O", 6), ("O", 5), ("O", 7), ("E", 5), ("E", 6), ("E", 7),
)
STARTS = tuple(sum(SIZES[:k]) for k in range(len(SIZES)))


def kernel(
    m_hbm, k_ref, out_ref,
    m_buf, k_pad, kbuf, kt, w_hi, w_lo, pbuf, p1s, p1r, r0, r1, r2, r3, ry,
    m_sem, ky_s, ky_r, kz_s, kz_r, kf_s, kf_r, p1_s, p1_rs, r1_s, r1_r, r2_s, r2_r, r3_s, r3_r, ry_s, ry_r, kg_s, kg_r, kd_s, kd_r,
):
    tm, space = lax.axis_index("tm"), lax.axis_index("space")
    z, yh, c = tm // 4, (tm // 2) % 2, tm % 2
    yl, x = space // NX, space % NX

    def at_z(step):
        return ((z + step + NZ) % NZ * 4 + yh * 2 + c, space)

    def at_x(step):
        return (tm, yl * NX + (x + step + NX) % NX)

    other_yh = (z * 4 + (1 - yh) * 2 + c, space)
    other_core = (z * 4 + yh * 2 + (1 - c), space)
    other_yl = (tm, (1 - yl) * NX + x)
    later, earlier = (tm + 2) % 32, (tm + 30) % 32
    has_later, has_earlier = tm < 30, tm >= 2
    mine = c * NZ

    barrier = pltpu.get_barrier_semaphore()
    greeted = [
        (later, space), (later, other_yl[1]), (earlier, space), (earlier, other_yl[1]),
        at_z(1), at_z(-1), at_x(1), at_x(-1), other_yh, other_core, other_yl,
    ]
    if "d" in GATHER:
        greeted = [at_z(4), at_z(3), at_z(-3), at_z(2), at_z(-2)] + greeted
    if "d" in REDUCE:
        greeted = [at_x(2)] + greeted
    for device in greeted:
        pl.semaphore_signal(barrier, inc=1, device_id=device, device_id_type=MESH)

    def load_model(i):
        rows = pl.ds(i * 256, 256)
        return pltpu.make_async_copy(m_hbm.at[rows], m_buf.at[rows], m_sem.at[i])

    for i in range(4):
        load_model(i).start()

    k_pad[...] = jnp.zeros_like(k_pad)
    for lag in range(LAGS):
        k_pad[lag, :, 0:600] = k_ref[lag]
    lane = lax.broadcasted_iota(jnp.int32, (32, 128), 1)
    for u in range(UNITS):
        base = min(UNIT * u // 128 * 128, 384)
        parts = []
        for lag in range(LAGS):
            shift = (UNIT * lag - (UNIT * u - base)) % 256
            wide = k_pad[lag, :, base : base + 256]
            parts.append((pltpu.roll(wide, shift, 1) if shift else wide)[:, 0:128])
        tile = jnp.where(lane < UNIT, parts[0], jnp.where(lane < 2 * UNIT, parts[1], parts[2]))
        kbuf[u, mine + z, yh] = tile
    pl.semaphore_wait(barrier, len(greeted))

    def remote(src, dst, send, recv, device):
        return pltpu.make_async_remote_copy(
            src_ref=src, dst_ref=dst, send_sem=send, recv_sem=recv, device_id=device, device_id_type=MESH
        )

    def units(k):
        return pl.ds(STARTS[k], SIZES[k])

    def rows(k):
        return pl.ds(STARTS[k] * UNIT, SIZES[k] * UNIT)

    def over_yh(k, half):
        block = kbuf.at[units(k), mine + z, half]
        return remote(block, block, ky_s.at[k], ky_r.at[k], other_yh)

    def over_z(k, hop, direction, source):
        sign = 1 - 2 * direction
        index = mine + (z - sign * source + NZ) % NZ
        if GATHER[k] == "g":
            block = kbuf.at[units(k), index, yh]
        else:
            block = kbuf.at[units(k), index] if hop < 4 else kbuf.at[units(k), index, direction]
        return remote(block, block, kz_s.at[k, direction, hop - 1], kz_r.at[k, direction, hop - 1], at_z(sign))

    def ring_over_yh(k, hop, direction, half):
        index = mine + (z - (1 - 2 * direction) * hop + NZ) % NZ
        block = kbuf.at[units(k), index, half]
        return remote(block, block, kg_s.at[k, direction, hop - 1], kg_r.at[k, direction, hop - 1], other_yh)

    def straight(k, mirrored, step, source, half):
        block = kbuf.at[units(k), mine + (z - source + NZ) % NZ, half]
        return remote(block, block, kd_s.at[k, mirrored, step - 1], kd_r.at[k, mirrored, step - 1], at_z(step))

    def ring_hops(k):
        return [(hop, direction) for hop in (1, 2, 3) for direction in (0, 1)] + [(4, k % 2)]

    def to_core(k, core):
        block = kbuf.at[units(k), pl.ds(core * NZ, NZ)]
        return remote(block, block, kf_s.at[k], kf_r.at[k], other_core)

    def swap_core(k, slot):
        return remote(
            p1s.at[slot, :, rows(k)], p1r.at[slot, :, rows(k)], p1_s.at[k, slot], p1_rs.at[k, slot], other_core
        )

    def over_yl(k, slot):
        return remote(
            pbuf.at[slot, 1 - yl, :, rows(k)], ry.at[slot, :, rows(k)], ry_s.at[k, slot], ry_r.at[k, slot], other_yl
        )

    def first_x(k, direction):
        if REDUCE[k] == "y":
            src, dst = pbuf.at[0, yl, direction, rows(k)], r1.at[direction, 0, rows(k)]
        else:
            src, dst = pbuf.at[0, direction, :, rows(k)], r1.at[direction, :, rows(k)]
        return remote(src, dst, r1_s.at[k, direction], r1_r.at[k, direction], at_x(1 - 2 * direction))

    def far_x(k):
        return remote(pbuf.at[0, :, :, rows(k)], r0.at[:, :, rows(k)], r1_s.at[k, 0], r1_r.at[k, 0], at_x(2))

    def second_x(k, direction):
        if REDUCE[k] == "y":
            src, dst = pbuf.at[1 + direction, yl, :, rows(k)], r2.at[direction, 0, :, rows(k)]
        else:
            src, dst = pbuf.at[1 + direction, :, :, rows(k)], r2.at[direction, :, :, rows(k)]
        return remote(src, dst, r2_s.at[k, direction], r2_r.at[k, direction], at_x(1 - 2 * direction))

    def last(k, which):
        src = (
            pbuf.at[3, 1 - yl, 0, rows(k)], pbuf.at[3, yl, 1, rows(k)], pbuf.at[3, 1 - yl, 1, rows(k)]
        )[which]
        device = (other_yl, (later, space), (later, other_yl[1]))[which]
        return remote(src, r3.at[which, rows(k)], r3_s.at[k, which], r3_r.at[k, which], device)

    def step_y(k):
        over_yh(k, yh).start()

    def step_h(k, hop):
        if GATHER[k] == "d":
            if hop == 2:
                over_yh(k, 1 - yh).wait_recv()
            for step in range(1, NZ):
                straight(k, hop - 1, step, 0, yh if hop == 1 else 1 - yh).start()
            return
        if GATHER[k] == "g":
            for direction in (0, 1):
                if (hop - 1, direction) in ring_hops(k):
                    over_z(k, hop - 1, direction, hop - 1).wait_recv()
                if (hop, direction) in ring_hops(k):
                    over_z(k, hop, direction, hop - 1).start()
                if (hop - 1, direction) in ring_hops(k):
                    ring_over_yh(k, hop - 1, direction, yh).start()
            return
        if hop == 1:
            over_yh(k, 1 - yh).wait_recv()
        for direction in (0, 1):
            if hop > 1:
                over_z(k, hop - 1, direction, hop - 1).wait_recv()
            over_z(k, hop, direction, hop - 1).start()

    def step_f(k):
        if GATHER[k] == "d":
            for mirrored in (0, 1):
                for step in range(1, NZ):
                    straight(k, mirrored, step, step, 1 - yh if mirrored else yh).wait_recv()
        elif GATHER[k] == "g":
            over_yh(k, 1 - yh).wait_recv()
            for hop, direction in ring_hops(k):
                ring_over_yh(k, hop, direction, 1 - yh).wait_recv()
        else:
            for direction in (0, 1):
                over_z(k, 4, direction, 4).wait_recv()
        to_core(k, c).start()

    def step_s(k):
        for i in range(4):
            load_model(i).wait()

        def split_rows(t, carry):
            part = m_buf[pl.ds(pl.multiple_of(t * 32, 32), 32), :]
            high = part.astype(BF16)
            low = (part - high.astype(F32)).astype(BF16)
            to = pl.ds(pl.multiple_of(((t % 2) * NZ + t // 4) * 64 + (t // 2) % 2 * 32, 32), 32)
            for d in range(NX):
                for half in (0, 1):
                    lanes = slice(half * 128, half * 128 + 128)
                    columns = slice(half * 512 + d * 128, half * 512 + d * 128 + 128)
                    w_hi[d, to, lanes] = high[:, columns]
                    w_lo[d, to, lanes] = low[:, columns]
            return carry

        lax.fori_loop(0, 32, split_rows, 0)

    def step_t(k):
        to_core(k, 1 - c).wait_recv()

        def block(b, carry):
            columns = pl.ds(pl.multiple_of(b * 128, 128), 128)
            for u in range(SIZES[k]):
                part = kbuf[STARTS[k] + u, pl.ds(2 * b, 2)].reshape(128, 128).T
                high = part.astype(BF16)
                low = (part - high.astype(F32)).astype(BF16)
                kt[u * 128 : (u + 1) * 128, columns] = high
                kt[(SIZES[k] + u) * 128 : (SIZES[k] + u + 1) * 128, columns] = low
            return carry

        lax.fori_loop(0, NZ, block, 0)

    def step_c(k, slot):
        to = (x + (2, 1, 3, 0)[slot]) % NX
        size = SIZES[k] * 128
        both = jnp.dot(kt[0 : 2 * size], w_hi[to], preferred_element_type=F32)
        acc = both[0:size] + both[size : 2 * size]
        acc = acc + jnp.dot(kt[0:size], w_lo[to], preferred_element_type=F32)
        for u in range(SIZES[k]):
            at = (STARTS[k] + u) * UNIT
            for half in (0, 1):
                lanes = slice(half * 128, half * 128 + 128)
                pbuf[slot, half, 0, at : at + UNIT] = acc[u * 128 : u * 128 + UNIT, lanes]
                p1s[slot, half, at : at + UNIT] = acc[u * 128 + UNIT : u * 128 + 2 * UNIT, lanes]
                pbuf[slot, half, 1, at : at + UNIT] = acc[u * 128 + 2 * UNIT : u * 128 + 3 * UNIT, lanes]
        swap_core(k, slot).start()

    def step_x(k, slot):
        swap_core(k, slot).wait_recv()
        for half in (0, 1):
            pbuf[slot, half, 1 - c, rows(k)] += p1r[slot, half, rows(k)]
        if REDUCE[k] == "y":
            over_yl(k, slot).start()

    def step_v(k, slot):
        over_yl(k, slot).wait_recv()
        pbuf[slot, yl, :, rows(k)] += ry[slot, :, rows(k)]

    def step_r1(k):
        if REDUCE[k] == "d":
            far_x(k).start()
            return
        for direction in (0, 1):
            first_x(k, direction).start()

    def step_r2(k):
        for direction in (0, 1):
            if REDUCE[k] == "d":
                second_x(k, direction).start()
                continue
            first_x(k, direction).wait_recv()
            if REDUCE[k] == "y":
                pbuf[1 + direction, yl, direction, rows(k)] += r1[direction, 0, rows(k)]
            else:
                pbuf[1 + direction, direction, :, rows(k)] += r1[direction, :, rows(k)]
            second_x(k, direction).start()

    def step_r3(k):
        for direction in (0, 1):
            second_x(k, direction).wait_recv()
        if REDUCE[k] == "y":
            pbuf[3, yl, :, rows(k)] = pbuf[3, yl, :, rows(k)] + r2[0, 0, :, rows(k)] + r2[1, 0, :, rows(k)]
        else:
            total = pbuf[3, :, :, rows(k)] + r2[0, :, :, rows(k)] + r2[1, :, :, rows(k)]
            if REDUCE[k] == "d":
                far_x(k).wait_recv()
                total = total + r0[:, :, rows(k)]
            pbuf[3, :, :, rows(k)] = total
            last(k, 0).start()

        @pl.when(has_later)
        def _():
            last(k, 1).start()
            if REDUCE[k] != "y":
                last(k, 2).start()

    def step_o(k):
        total = pbuf[3, yl, 0, rows(k)]
        if REDUCE[k] != "y":
            last(k, 0).wait_recv()
            total = total + r3[0, rows(k)]
        out_ref[rows(k)] = total

        @pl.when(has_earlier)
        def _():
            last(k, 1).wait_recv()
            more = r3[1, rows(k)]
            if REDUCE[k] != "y":
                last(k, 2).wait_recv()
                more = more + r3[2, rows(k)]
            out_ref[rows(k)] += more

    def step_d(k):
        over_yh(k, yh).wait_send()
        if GATHER[k] == "d":
            for mirrored in (0, 1):
                for step in range(1, NZ):
                    straight(k, mirrored, step, 0, 1 - yh if mirrored else yh).wait_send()
        elif GATHER[k] == "g":
            for hop, direction in ring_hops(k):
                over_z(k, hop, direction, hop - 1).wait_send()
                ring_over_yh(k, hop, direction, yh).wait_send()
        else:
            for direction in (0, 1):
                for hop in (1, 2, 3, 4):
                    over_z(k, hop, direction, hop - 1).wait_send()
        if REDUCE[k] == "d":
            far_x(k).wait_send()
        for direction in (0, 1):
            if REDUCE[k] != "d":
                first_x(k, direction).wait_send()
            second_x(k, direction).wait_send()
        to_core(k, c).wait_send()
        for slot in range(4):
            swap_core(k, slot).wait_send()
            if REDUCE[k] == "y":
                over_yl(k, slot).wait_send()

    def step_e(k):
        if REDUCE[k] != "y":
            last(k, 0).wait_send()

        @pl.when(has_later)
        def _():
            last(k, 1).wait_send()
            if REDUCE[k] != "y":
                last(k, 2).wait_send()

    steps = {
        "Y": step_y, "F": step_f, "S": step_s, "T": step_t, "R1": step_r1, "R2": step_r2, "R3": step_r3,
        "O": step_o, "D": step_d, "E": step_e,
    }
    for hop in (1, 2, 3, 4, 5):
        steps[f"H{hop}"] = functools.partial(step_h, hop=hop)
    for slot in range(4):
        steps[f"C{slot}"] = functools.partial(step_c, slot=slot)
        steps[f"X{slot}"] = functools.partial(step_x, slot=slot)
        steps[f"V{slot}"] = functools.partial(step_v, slot=slot)
    for name, k in ORDER:
        steps[name](k)


def on_device(model, kernels):
    dma, vmem, n = pltpu.SemaphoreType.DMA, pltpu.VMEM, len(SIZES)
    result = pl.pallas_call(
        kernel,
        out_shape=jax.ShapeDtypeStruct((600, 128), F32),
        in_specs=[pl.BlockSpec(memory_space=pl.ANY), pl.BlockSpec(memory_space=pltpu.VMEM)],
        out_specs=pl.BlockSpec(memory_space=pltpu.VMEM),
        scratch_shapes=[
            vmem((1024, 1024), F32),
            vmem((LAGS, 32, 640), F32),
            vmem((UNITS, 2 * NZ, 2, 32, 128), F32),
            vmem((max(SIZES) * 256, 1024), BF16),
            vmem((NX, 1024, 256), BF16),
            vmem((NX, 1024, 256), BF16),
            vmem((4, 2, 2, 600, 128), F32),
            vmem((4, 2, 600, 128), F32),
            vmem((4, 2, 600, 128), F32),
            vmem((2, 2, 600, 128), F32),
            vmem((2, 2, 600, 128), F32),
            vmem((2, 2, 2, 600, 128), F32),
            vmem((3, 600, 128), F32),
            vmem((4, 2, 600, 128), F32),
            dma((4,)),
            dma((n,)), dma((n,)),
            dma((n, 2, 4)), dma((n, 2, 4)),
            dma((n,)), dma((n,)),
            dma((n, 4)), dma((n, 4)),
            dma((n, 2)), dma((n, 2)),
            dma((n, 2)), dma((n, 2)),
            dma((n, 3)), dma((n, 3)),
            dma((n, 4)), dma((n, 4)),
            dma((n, 2, 4)), dma((n, 2, 4)),
            dma((n, 2, 7)), dma((n, 2, 7)),
        ],
        compiler_params=pltpu.CompilerParams(
            collective_id=0, has_side_effects=True, vmem_limit_bytes=60 * 1024 * 1024
        ),
        name="toeplitz",
    )(model[0], jnp.swapaxes(kernels, 1, 2))
    return result[None]


def solution(mesh):
    return jax.shard_map(
        on_device,
        mesh=mesh,
        in_specs=(P("tm", "space", None), P(None, None, ("space", "tm"))),
        out_specs=P("tm", None, "space"),
        check_vma=False,
    )
```
